32 devices in a mesh: row: 16 (over z, y, core), col: 2 (over x).
Axes of the slice: x: 2, y: 2, z: 4, core: 2. Of those that a mesh axis runs over, the one named last changes fastest.
Arguments:
- views: bfloat16 [81, 1024, 512], P(None, 'row', 'col'), may hold values from -6 to 6
Outputs:
- increment: float32 [1024, 512], P('row', 'col')
- residual: float32 [1024, 512], P('row', 'col')
The draws below stay inside these ranges and needn't reach their ends.
All inputs are finite; a program needn't handle non-finite values.
Results may differ from the reference program's by a relative error of at most 0.0005.
Values may be sent and summed in bfloat16 or wider, within the bound.
A program may use at most 64 MiB of HBM per device.

```python
import jax
import jax.numpy as jnp

ANG = 9
VIEWS = 81
D0 = 3
HALO = 13
ITERS = 2
NR = 1024
NC = 512


def levels(own_key, extent, split, least, high):
    factor_of = 1.0
    for axis_at, shards_of in split:
        draws = jax.random.uniform(jax.random.fold_in(jax.random.fold_in(own_key, 6), axis_at), (shards_of,), jnp.float32, least / len(split), high / len(split))
        factor_of = factor_of * jnp.repeat(jnp.exp(draws), extent[axis_at] // shards_of).reshape((-1,) + (1,) * (len(extent) - 1 - axis_at))
    return factor_of


def scatter_about(own_key, dims, scale, most, cuts=(), kind=jnp.bfloat16):
    loudness = levels(own_key, dims, cuts, -0.22, 0.18) if cuts else 1.0
    result = jax.random.normal(own_key, dims, jnp.float32) * scale * loudness
    return jnp.minimum(jnp.maximum(result, -most), most).astype(kind)


def setup_inputs(seed: int = 0) -> dict:
    key_of = jax.random.split(jax.random.key(seed), 2)
    views = scatter_about(key_of[0], (VIEWS, NR, NC), 1.0, 6.0, ((1, 16), (2, 2)))
    return {"views": views}


smooth_weight = 2.0
damping = 0.1

def edge_weights(center):
    padded = jnp.pad(center, 1)
    across = padded[1:-1, 1:] - padded[1:-1, :-1]
    vertical = padded[1:, 1:-1] - padded[:-1, 1:-1]
    columns = jnp.arange(NC + 1)
    row_index = jnp.arange(NR + 1)
    horiz = jnp.where(((columns >= 1) & (columns <= NC - 1))[None, :], jnp.exp(-across * across), 0.0)
    verti = jnp.where(((row_index >= 1) & (row_index <= NR - 1))[:, None], jnp.exp(-vertical * vertical), 0.0)
    return (horiz, verti)

def apply_operator(field, coeff, horiz, verti):
    padded = jnp.pad(field, 1)
    edges = horiz[:, 1:] * (field - padded[1:-1, 2:]) + horiz[:, :-1] * (field - padded[1:-1, :-2])
    edges = edges + verti[1:] * (field - padded[2:, 1:-1]) + verti[:-1] * (field - padded[:-2, 1:-1])
    return coeff * field + smooth_weight * edges

def reference(views):
    padded = jnp.pad(views, ((0, 0), (HALO, HALO), (HALO, HALO)))
    center = views[VIEWS // 2].astype(jnp.float32)
    data_sum = jnp.zeros((NR, NC), jnp.float32)
    source_sum = jnp.zeros((NR, NC), jnp.float32)
    for index in range(VIEWS):
        srow = index // ANG - ANG // 2
        tcol = index % ANG - ANG // 2
        top = HALO + D0 * srow
        left = HALO + D0 * tcol
        image = padded[index].astype(jnp.float32)
        warped = image[top:top + NR, left:left + NC]
        down_diff = 0.5 * (image[top + 1:top + 1 + NR, left:left + NC] - image[top - 1:top - 1 + NR, left:left + NC])
        side_diff = 0.5 * (image[top:top + NR, left + 1:left + 1 + NC] - image[top:top + NR, left - 1:left - 1 + NC])
        slope = srow * down_diff + tcol * side_diff
        error = warped - center
        robust = 1.0 / jnp.sqrt(1.0 + error * error)
        data_sum = data_sum + robust * slope * slope
        source_sum = source_sum - robust * slope * error
    coeff = damping + data_sum / VIEWS
    source = source_sum / VIEWS
    horiz, verti = edge_weights(center)
    precond = coeff + smooth_weight * (horiz[:, 1:] + horiz[:, :-1] + verti[1:] + verti[:-1])
    solution = jnp.zeros_like(source)
    residual = source
    zed = residual / precond
    direction = zed
    inner_now = jnp.sum(residual * zed)
    for step in range(ITERS):
        image_dir = apply_operator(direction, coeff, horiz, verti)
        step_size = inner_now / jnp.sum(direction * image_dir)
        solution = solution + step_size * direction
        residual = residual - step_size * image_dir
        zed = residual / precond
        inner_next = jnp.sum(residual * zed)
        direction = zed + inner_next / inner_now * direction
        inner_now = inner_next
    return (solution, residual)
```

```python
import functools

import jax
import jax.numpy as jnp
from jax import lax
from jax.experimental import pallas as pl
from jax.experimental.pallas import tpu as pltpu
from jax.sharding import PartitionSpec as P

ANG = 9
VIEWS = 81
HALF = 4
CENTER = 40
D0 = 3
smooth_weight = 2.0
damping = 0.1
PAD = 16
LANES = 128
F32 = jnp.float32
DIRS = ((-1, 0), (1, 0), (0, -1), (0, 1), (-1, -1), (-1, 1), (1, -1), (1, 1))


def roll(x, shift):
    return pltpu.roll(x, shift % LANES, 1)


def lane_of(rows):
    return lax.broadcasted_iota(jnp.int32, (rows, LANES), 1)


def kernel(nrow, ncol, views, inc, res, ext, sp, col_r, col_l, fb, pb, cen, cpack, acc, pacc, own, zc, gpack,
           ghost_u, ghost_d, ghost_l, ghost_r, corner, redbuf, redout, load_sem, send1, recv1, send2, recv2, rsend, rrecv):
    rows, cols = views.shape[1], views.shape[2]
    r, c = lax.axis_index("row"), lax.axis_index("col")
    count = nrow * ncol
    me = r * ncol + c
    full = PAD + rows + PAD

    def exists(dr, dc):
        return (r + dr >= 0) & (r + dr < nrow) & (c + dc >= 0) & (c + dc < ncol)

    barrier = pltpu.get_barrier_semaphore()

    def greet(i, carry):
        peer = (me + i) % count
        pl.semaphore_signal(barrier, inc=1, device_id=(peer // ncol, peer % ncol), device_id_type=pl.DeviceIdType.MESH)
        return carry

    lax.fori_loop(1, count, greet, 0)

    loads = []
    for si in range(ANG):
        part = pl.ds(si * ANG, ANG)
        copy = pltpu.make_async_copy(views.at[part], ext.at[part, pl.ds(PAD, rows), :], load_sem.at[si])
        copy.start()
        loads.append(copy)

    def zero(ref, first, number, row, size):
        def body(i, carry):
            ref[first + i, row : row + size, :] = jnp.zeros((size, ref.shape[2]), ref.dtype)
            return carry
        lax.fori_loop(0, number, body, 0)

    @pl.when(r == 0)
    def _():
        zero(ext, 0, 41, 0, PAD)

    @pl.when(r == nrow - 1)
    def _():
        zero(ext, 40, 41, PAD + rows, PAD)

    for ref, edge in ((col_r, c == ncol - 1), (col_l, c == 0)):
        @pl.when(edge)
        def _():
            zero(ref, 0, 10, PAD, rows)

        @pl.when(edge | (r == 0))
        def _():
            zero(ref, 0, 6, 0, PAD)

        @pl.when(edge | (r == nrow - 1))
        def _():
            zero(ref, 5, 5, PAD + rows, PAD)

    for edge, ref in ((r == 0, ghost_u), (r == nrow - 1, ghost_d)):
        @pl.when(edge)
        def _():
            ref[0] = jnp.zeros((8, cols), F32)
            ref[1] = jnp.ones((8, cols), F32)
    for edge, ref, low in ((c == 0, ghost_l, 1.0), (c == ncol - 1, ghost_r, 0.0)):
        @pl.when(edge)
        def _():
            ref[...] = jnp.where(lane_of(rows) < 64, low, 1.0 - low)
    for index, (dr, dc) in enumerate(DIRS[4:]):
        @pl.when(jnp.logical_not(exists(-dr, -dc)))
        def _():
            corner[index] = jnp.zeros((8, LANES), F32)

    pl.semaphore_wait(barrier, count - 1)

    up_rows, down_rows = pl.ds(0, PAD), pl.ds(rows - PAD, PAD)
    copies = []
    for index, (dr, dc) in enumerate(DIRS):
        if dc == 0:
            if dr < 0:
                src, dst = views.at[pl.ds(40, 41), up_rows, :], ext.at[pl.ds(40, 41), pl.ds(PAD + rows, PAD), :]
            else:
                src, dst = views.at[pl.ds(0, 41), down_rows, :], ext.at[pl.ds(0, 41), pl.ds(0, PAD), :]
        else:
            side = col_r if dc < 0 else col_l
            if dr == 0:
                src, dst = sp, side.at[:, pl.ds(PAD, rows), :]
            elif dr < 0:
                src, dst = sp.at[pl.ds(5, 5), up_rows, :], side.at[pl.ds(5, 5), pl.ds(PAD + rows, PAD), :]
            else:
                src, dst = sp.at[pl.ds(0, 6), down_rows, :], side.at[pl.ds(0, 6), pl.ds(0, PAD), :]
        copies.append((dr, dc, pltpu.make_async_remote_copy(
            src_ref=src, dst_ref=dst, send_sem=send1.at[index], recv_sem=recv1.at[index],
            device_id=(r + dr, c + dc), device_id_type=pl.DeviceIdType.MESH)))

    def start(group):
        for dr, dc, copy in group:
            @pl.when(exists(dr, dc))
            def _():
                copy.start()

    def arrive(group):
        for dr, dc, copy in group:
            @pl.when(exists(-dr, -dc))
            def _():
                copy.wait_recv()

    def drain(group):
        for dr, dc, copy in group:
            @pl.when(exists(dr, dc))
            def _():
                copy.wait_send()

    start(copies[:2])
    for copy in loads:
        copy.wait()

    lane = lane_of(rows)
    group = (lane % 64) // 16
    place = lane % 16
    right_part = lane < 64

    def pack(si, carry):
        total = jnp.zeros((rows, LANES), F32)
        for g in range(HALF):
            a = ext[si * ANG + HALF + g + 1, PAD : PAD + rows, 0:LANES].astype(F32)
            b = ext[si * ANG + HALF - g - 1, PAD : PAD + rows, cols - LANES : cols].astype(F32)
            total = jnp.where(right_part & (group == g), roll(a, 16 * g + 2), total)
            total = jnp.where((~right_part) & (group == g), roll(b, 16 * g + 78), total)
        sp[si + (si + 3) // 8] = total.astype(sp.dtype)
        return carry

    lax.fori_loop(0, ANG, pack, 0)
    sp[5] = jnp.where(right_part, ext[CENTER, PAD : PAD + rows, 0:LANES].astype(F32),
                      ext[CENTER, PAD : PAD + rows, cols - LANES : cols].astype(F32)).astype(sp.dtype)
    start(copies[2:])

    center = [ext[CENTER, PAD : PAD + rows, h * LANES : (h + 1) * LANES].astype(F32) for h in range(2)]
    ca, cb = center
    for ti in range(ANG):
        move = D0 * (ti - HALF)
        ra, rb = roll(ca, move), roll(cb, move)
        if move > 0:
            cen[ti, 0] = ra
            cen[ti, 1] = jnp.where(lane >= move, rb, ra)
        elif move < 0:
            cen[ti, 0] = jnp.where(lane < LANES + move, ra, rb)
            cen[ti, 1] = rb
        else:
            cen[ti, 0] = ca
            cen[ti, 1] = cb
    total = jnp.zeros((rows, LANES), F32)
    for g in range(HALF):
        m = D0 * (g + 1)
        total = jnp.where(right_part & (group == g), roll(cb, 16 * g - 126 + m), total)
        total = jnp.where((~right_part) & (group == g), roll(ca, 78 + 16 * g - m), total)
    cpack[...] = total
    pacc[...] = jnp.zeros_like(pacc)

    chunk = 16
    clane = lane_of(chunk)

    def terms(v0, side, down, s, tscale, middle):
        slope = tscale * side if s == 0 else (0.5 * s) * down + tscale * side
        error = v0 - middle
        weighted = slope * lax.rsqrt(1.0 + error * error)
        return weighted * slope, weighted * error

    def view_pass(signs):
        def body(ti, carry):
            tscale = 0.5 * (ti - HALF).astype(F32)
            for slot, s in enumerate(signs):
                low = 0 if s < 0 else PAD
                size = rows if s == 0 else rows + PAD
                for h in range(2):
                    fb[slot, h, low : low + size, :] = ext[
                        ANG * (s + HALF) + ti, low : low + size, h * LANES : (h + 1) * LANES].astype(F32)
            for at in range(0, rows, chunk):
                sums = [[None, None], [None, None]]
                middle = [cen[ti, h, at : at + chunk, :] for h in range(2)]
                for slot, s in enumerate(signs):
                    base = PAD + D0 * s + at
                    v0 = [fb[slot, h, base : base + chunk, :] for h in range(2)]
                    after = [roll(v, -1) for v in v0]
                    before = [roll(v, 1) for v in v0]
                    after[0] = jnp.where(clane == LANES - 1, after[1], after[0])
                    before[1] = jnp.where(clane == 0, before[0], before[1])
                    for h in range(2):
                        down = None
                        if s:
                            down = fb[slot, h, base + 1 : base + 1 + chunk, :] - fb[slot, h, base - 1 : base - 1 + chunk, :]
                        data, src = terms(v0[h], after[h] - before[h], down, s, tscale, middle[h])
                        sums[0][h] = data if sums[0][h] is None else sums[0][h] + data
                        sums[1][h] = src if sums[1][h] is None else sums[1][h] + src
                for f in range(2):
                    for h in range(2):
                        old = sums[f][h] if signs == (0,) else acc[ti, f, h, at : at + chunk, :] + sums[f][h]
                        acc[ti, f, h, at : at + chunk, :] = old
            return carry

        lax.fori_loop(0, ANG, body, 0)

    view_pass((0,))
    arrive(copies)
    for size in range(1, HALF + 1):
        view_pass((size, -size))

    flane = lane_of(full)
    fgroup, fplace, fright = (flane % 64) // 16, flane % 16, flane < 64
    ptscale = jnp.where(clane < 64, 0.5, -0.5) * ((clane % 64) // 16 + 1).astype(F32)
    for si in range(ANG):
        s = si - HALF
        slot = si + (si + 3) // 8
        low = 0 if s < 0 else PAD
        size = rows if s == 0 else rows + PAD
        part = slice(low, low + size)
        right, grp, plc = fright[part], fgroup[part], fplace[part]
        merged = jnp.where(right, col_r[slot, part, :].astype(F32), col_l[slot, part, :].astype(F32))
        for g in range(HALF):
            a = ext[si * ANG + HALF - g - 1, part, 0:LANES].astype(F32)
            b = ext[si * ANG + HALF + g + 1, part, cols - LANES : cols].astype(F32)
            merged = jnp.where(right & (grp == g) & (plc < 2), roll(b, 16 * g + 2), merged)
            merged = jnp.where((~right) & (grp == g) & (plc >= 14), roll(a, 16 * g + 78), merged)
        pb[part, :] = merged
        for at in range(0, rows, chunk):
            base = PAD + D0 * s + at
            v0 = pb[base : base + chunk, :]
            down = pb[base + 1 : base + 1 + chunk, :] - pb[base - 1 : base - 1 + chunk, :] if s else None
            data, src = terms(v0, roll(v0, -1) - roll(v0, 1), down, s, ptscale, cpack[at : at + chunk, :])
            pacc[0, at : at + chunk, :] += data
            pacc[1, at : at + chunk, :] += src

    for f in range(2):
        ta, tb = acc[HALF, f, 0], acc[HALF, f, 1]
        for ti in range(ANG):
            m = D0 * abs(ti - HALF)
            if m == 0:
                continue
            a, b = acc[ti, f, 0], acc[ti, f, 1]
            g = m // D0 - 1
            if ti > HALF:
                ra, rb = roll(a, -m), roll(b, -m)
                ta = ta + jnp.where(lane < LANES - m, ra, rb)
                tb = tb + jnp.where(lane <= LANES - 2 - m, rb, roll(pacc[f], 126 - m - 16 * g))
            else:
                ra, rb = roll(a, m), roll(b, m)
                ta = ta + jnp.where(lane >= m + 1, ra, roll(pacc[f], m - 78 - 16 * g))
                tb = tb + jnp.where(lane >= m, rb, ra)
        own[f, :, 0:LANES] = ta
        own[f, :, LANES : 2 * LANES] = tb

    coeff = damping + own[0] * (1.0 / VIEWS)
    source = own[1] * (-1.0 / VIEWS)

    frows, fcols = rows + 16, cols + 2 * LANES
    top = jnp.concatenate([col_l[5, 0:PAD, :], ext[CENTER, 0:PAD, :], col_r[5, 0:PAD, :]], axis=1).astype(F32)[8:16]
    mid = jnp.concatenate([col_l[5, PAD : PAD + rows, :], ext[CENTER, PAD : PAD + rows, :], col_r[5, PAD : PAD + rows, :]], axis=1).astype(F32)
    bot = jnp.concatenate([col_l[5, PAD + rows : full, :], ext[CENTER, PAD + rows : full, :], col_r[5, PAD + rows : full, :]], axis=1).astype(F32)[0:8]
    cf = jnp.concatenate([top, mid, bot], axis=0)
    gcol = lax.broadcasted_iota(jnp.int32, (frows, fcols), 1) + (c * cols - LANES)
    grow = lax.broadcasted_iota(jnp.int32, (frows, fcols), 0) + (r * rows - 8)

    def east(x):
        return pltpu.roll(x, fcols - 1, 1)

    def west(x):
        return pltpu.roll(x, 1, 1)

    def south(x):
        return pltpu.roll(x, frows - 1, 0)

    def north(x):
        return pltpu.roll(x, 1, 0)

    dx = east(cf) - cf
    dy = south(cf) - cf
    edge_e = jnp.where((gcol >= 0) & (gcol < ncol * cols - 1), jnp.exp(-dx * dx), 0.0)
    edge_s = jnp.where((grow >= 0) & (grow < nrow * rows - 1), jnp.exp(-dy * dy), 0.0)
    edge_w, edge_n = west(edge_e), north(edge_s)
    weights = smooth_weight * (edge_e + edge_w + edge_s + edge_n)

    inner = (slice(8, 8 + rows), slice(LANES, LANES + cols))
    zed = source / (coeff + weights[inner])
    zc[0] = zed
    zc[1] = coeff
    gpack[0] = jnp.where(right_part, zed[:, 0:LANES], roll(coeff[:, 0:LANES], 64))
    gpack[1] = jnp.where(right_part, roll(coeff[:, cols - LANES : cols], 64), zed[:, cols - LANES : cols])

    copies2 = []
    for index, (dr, dc) in enumerate(DIRS):
        if dc == 0:
            src = zc.at[:, pl.ds(0, 8), :] if dr < 0 else zc.at[:, pl.ds(rows - 8, 8), :]
            dst = ghost_d if dr < 0 else ghost_u
        elif dr == 0:
            src = gpack.at[0] if dc < 0 else gpack.at[1]
            dst = ghost_r if dc < 0 else ghost_l
        else:
            src = gpack.at[0 if dc < 0 else 1, pl.ds(0 if dr < 0 else rows - 8, 8), :]
            dst = corner.at[index - 4]
        copies2.append((dr, dc, pltpu.make_async_remote_copy(
            src_ref=src, dst_ref=dst, send_sem=send2.at[index], recv_sem=recv2.at[index],
            device_id=(r + dr, c + dc), device_id_type=pl.DeviceIdType.MESH)))
    start(copies2)
    drain(copies)
    arrive(copies2)

    zf = jnp.concatenate([
        jnp.concatenate([corner[3], ghost_u[0], corner[2]], axis=1),
        jnp.concatenate([ghost_l[...], zed, ghost_r[...]], axis=1),
        jnp.concatenate([corner[1], ghost_d[0], corner[0]], axis=1)], axis=0)
    one = jnp.ones((8, LANES), F32)
    kf = jnp.concatenate([
        jnp.concatenate([one, ghost_u[1], one], axis=1),
        jnp.concatenate([roll(ghost_l[...], 64), coeff, roll(ghost_r[...], 64)], axis=1),
        jnp.concatenate([one, ghost_d[1], one], axis=1)], axis=0)
    diag = kf + weights

    def operate(z):
        edges = edge_e * east(z) + edge_w * west(z) + edge_s * south(z) + edge_n * north(z)
        return diag * z - smooth_weight * edges

    wf = operate(zf)
    qf = wf / diag
    vf = operate(qf)
    w, q, v = wf[inner], qf[inner], vf[inner]
    rest = source - w
    y = zed - q
    wv = w - v
    sums = (zed * w, zed * rest, y * rest, q * rest, q * w, y * wv, y * v, q * v)
    line = lax.broadcasted_iota(jnp.int32, (1, LANES), 1)
    packed = jnp.zeros((1, LANES), F32)
    for i, x in enumerate(sums):
        x = jnp.sum(x, axis=0, keepdims=True)
        x = jnp.sum(x, axis=1, keepdims=True)
        packed = jnp.where(line == i, x, packed)
    redout[0] = packed
    redbuf[me] = packed

    def red_copy(i):
        peer = (me + i) % count
        return pltpu.make_async_remote_copy(
            src_ref=redout.at[0], dst_ref=redbuf.at[me], send_sem=rsend.at[0], recv_sem=rrecv.at[0],
            device_id=(peer // ncol, peer % ncol), device_id_type=pl.DeviceIdType.MESH)

    def cast_out(i, carry):
        red_copy(i).start()
        return carry

    lax.fori_loop(1, count, cast_out, 0)
    drain(copies2)
    others = redbuf.at[pl.ds(0, count - 1)]
    pltpu.make_async_copy(others, others, rrecv.at[0]).wait()
    pltpu.make_async_copy(others, others, rsend.at[0]).wait()
    totals = jnp.sum(redbuf[...], axis=0)
    b, e, f, g, h, k, l, m = [totals[:, i : i + 1] for i in range(8)]
    delta = e / b
    step0 = (e + b) / b
    rz0 = e + b
    rz1 = f - 2.0 * delta * g + delta * delta * h
    wu1 = k - 2.0 * delta * l + delta * delta * m
    beta = rz1 / rz0
    step1 = rz1 / (wu1 - beta * rz1 / step0)
    direction = (y - delta * q) + beta * zed
    image = (wv - delta * v) + beta * w
    inc[...] = step0 * zed + step1 * direction
    res[...] = (source - step0 * w) - step1 * image


def solution(mesh):
    nrow, ncol = mesh.shape["row"], mesh.shape["col"]

    def shards(views):
        _, rows, cols = views.shape
        full = PAD + rows + PAD
        bf = views.dtype
        return pl.pallas_call(
            functools.partial(kernel, nrow, ncol),
            out_shape=(jax.ShapeDtypeStruct((rows, cols), F32),) * 2,
            in_specs=[pl.BlockSpec(memory_space=pl.ANY)],
            out_specs=[pl.BlockSpec(memory_space=pltpu.VMEM)] * 2,
            scratch_shapes=[
                pltpu.VMEM((VIEWS, full, cols), bf),
                pltpu.VMEM((10, rows, LANES), bf),
                pltpu.VMEM((10, full, LANES), bf),
                pltpu.VMEM((10, full, LANES), bf),
                pltpu.VMEM((2, 2, full, LANES), F32),
                pltpu.VMEM((full, LANES), F32),
                pltpu.VMEM((ANG, 2, rows, LANES), F32),
                pltpu.VMEM((rows, LANES), F32),
                pltpu.VMEM((ANG, 2, 2, rows, LANES), F32),
                pltpu.VMEM((2, rows, LANES), F32),
                pltpu.VMEM((2, rows, cols), F32),
                pltpu.VMEM((2, rows, cols), F32),
                pltpu.VMEM((2, rows, LANES), F32),
                pltpu.VMEM((2, 8, cols), F32),
                pltpu.VMEM((2, 8, cols), F32),
                pltpu.VMEM((rows, LANES), F32),
                pltpu.VMEM((rows, LANES), F32),
                pltpu.VMEM((4, 8, LANES), F32),
                pltpu.VMEM((nrow * ncol, 1, LANES), F32),
                pltpu.VMEM((1, 1, LANES), F32),
                pltpu.SemaphoreType.DMA((ANG,)),
                pltpu.SemaphoreType.DMA((8,)),
                pltpu.SemaphoreType.DMA((8,)),
                pltpu.SemaphoreType.DMA((8,)),
                pltpu.SemaphoreType.DMA((8,)),
                pltpu.SemaphoreType.DMA((1,)),
                pltpu.SemaphoreType.DMA((1,)),
            ],
            compiler_params=pltpu.CompilerParams(collective_id=0, has_side_effects=True, vmem_limit_bytes=48 << 20),
        )(views)

    return jax.shard_map(
        shards,
        mesh=mesh,
        in_specs=(P(None, "row", "col"),),
        out_specs=(P("row", "col"), P("row", "col")),
        check_vma=False,
    )
```

```python
import functools

import jax
import jax.numpy as jnp
from jax import lax
from jax.experimental import pallas as pl
from jax.experimental.pallas import tpu as pltpu
from jax.sharding import PartitionSpec as P

ANG = 9
VIEWS = 81
HALF = 4
CENTER = 40
D0 = 3
smooth_weight = 2.0
damping = 0.1
PAD = 16
LANES = 128
F32 = jnp.float32
DIRS = ((-1, 0), (1, 0), (0, -1), (0, 1), (-1, -1), (-1, 1), (1, -1), (1, 1))


def roll(x, shift):
    return pltpu.roll(x, shift % LANES, 1)


def lane_of(rows):
    return lax.broadcasted_iota(jnp.int32, (rows, LANES), 1)


def kernel(nrow, ncol, views, inc, res, ext, sp, col_r, col_l, fb, pb, cen, cpack, acc, pacc, own, zc, gpack,
           ghost_u, ghost_d, ghost_l, ghost_r, corner, redbuf, redout, load_sem, send1, recv1, send2, recv2, rsend, rrecv):
    rows, cols = views.shape[1], views.shape[2]
    r, c = lax.axis_index("row"), lax.axis_index("col")
    count = nrow * ncol
    me = r * ncol + c
    full = PAD + rows + PAD

    def exists(dr, dc):
        return (r + dr >= 0) & (r + dr < nrow) & (c + dc >= 0) & (c + dc < ncol)

    barrier = pltpu.get_barrier_semaphore()

    def greet(i, carry):
        peer = (me + i) % count
        pl.semaphore_signal(barrier, inc=1, device_id=(peer // ncol, peer % ncol), device_id_type=pl.DeviceIdType.MESH)
        return carry

    lax.fori_loop(1, count, greet, 0)

    loads = []
    for si in range(ANG):
        part = pl.ds(si * ANG, ANG)
        copy = pltpu.make_async_copy(views.at[part], ext.at[part, pl.ds(PAD, rows), :], load_sem.at[si])
        copy.start()
        loads.append(copy)

    def zero(ref, first, number, row, size):
        def body(i, carry):
            ref[first + i, row : row + size, :] = jnp.zeros((size, ref.shape[2]), ref.dtype)
            return carry
        lax.fori_loop(0, number, body, 0)

    @pl.when(r == 0)
    def _():
        zero(ext, 0, 41, 0, PAD)

    @pl.when(r == nrow - 1)
    def _():
        zero(ext, 40, 41, PAD + rows, PAD)

    for ref, edge in ((col_r, c == ncol - 1), (col_l, c == 0)):
        @pl.when(edge)
        def _():
            zero(ref, 0, 5, PAD, rows)

        @pl.when(edge | (r == 0))
        def _():
            zero(ref, 0, 3, 0, PAD)

        @pl.when(edge | (r == nrow - 1))
        def _():
            zero(ref, 2, 3, PAD + rows, PAD)

    for edge, ref in ((r == 0, ghost_u), (r == nrow - 1, ghost_d)):
        @pl.when(edge)
        def _():
            ref[0] = jnp.zeros((8, cols), F32)
            ref[1] = jnp.ones((8, cols), F32)
    for edge, ref, low in ((c == 0, ghost_l, 1.0), (c == ncol - 1, ghost_r, 0.0)):
        @pl.when(edge)
        def _():
            ref[...] = jnp.where(lane_of(rows) < 64, low, 1.0 - low)
    for index, (dr, dc) in enumerate(DIRS[4:]):
        @pl.when(jnp.logical_not(exists(-dr, -dc)))
        def _():
            corner[index] = jnp.zeros((8, LANES), F32)

    pl.semaphore_wait(barrier, count - 1)

    row_copies = []
    for size in range(HALF + 1):
        reach = 8 if D0 * size + 1 <= 8 else PAD
        for index, (dr, dc) in enumerate(DIRS[:2]):
            if size == 0:
                part = pl.ds(CENTER, 1)
            else:
                part = pl.ds(ANG * (HALF - dr * size), ANG)
            if dr < 0:
                src, dst = views.at[part, pl.ds(0, reach), :], ext.at[part, pl.ds(PAD + rows, reach), :]
            else:
                src, dst = views.at[part, pl.ds(rows - reach, reach), :], ext.at[part, pl.ds(PAD - reach, reach), :]
            row_copies.append((dr, dc, pltpu.make_async_remote_copy(
                src_ref=src, dst_ref=dst, send_sem=send1.at[2 * size + index], recv_sem=recv1.at[2 * size + index],
                device_id=(r + dr, c + dc), device_id_type=pl.DeviceIdType.MESH)))
    col_copies = []
    for index, (dr, dc) in enumerate(DIRS[2:]):
        side = col_r if dc < 0 else col_l
        mine = sp.at[0 if dc < 0 else 1]
        if dr == 0:
            src, dst = mine, side.at[:, pl.ds(PAD, rows), :]
        elif dr < 0:
            src, dst = mine.at[pl.ds(2, 3), pl.ds(0, PAD), :], side.at[pl.ds(2, 3), pl.ds(PAD + rows, PAD), :]
        else:
            src, dst = mine.at[pl.ds(0, 3), pl.ds(rows - PAD, PAD), :], side.at[pl.ds(0, 3), pl.ds(0, PAD), :]
        col_copies.append((dr, dc, pltpu.make_async_remote_copy(
            src_ref=src, dst_ref=dst, send_sem=send1.at[10 + index], recv_sem=recv1.at[10 + index],
            device_id=(r + dr, c + dc), device_id_type=pl.DeviceIdType.MESH)))

    def start(group):
        for dr, dc, copy in group:
            @pl.when(exists(dr, dc))
            def _():
                copy.start()

    def arrive(group):
        for dr, dc, copy in group:
            @pl.when(exists(-dr, -dc))
            def _():
                copy.wait_recv()

    def drain(group):
        for dr, dc, copy in group:
            @pl.when(exists(dr, dc))
            def _():
                copy.wait_send()

    start(row_copies)
    for copy in loads:
        copy.wait()

    lane = lane_of(rows)
    group = (lane % 64) // 16
    place = lane % 16
    right_part = lane < 64

    for slot in range(5):
        left = right = None
        for half in range(2):
            if slot == 2 and half == 1:
                a = roll(ext[CENTER, PAD : PAD + rows, 0:LANES].astype(F32), 64)
                b = ext[CENTER, PAD : PAD + rows, cols - LANES : cols].astype(F32)
            else:
                si = (0, 2, 4, 5, 7)[slot] + half
                a = b = None
                for g in range(HALF):
                    x = ext[si * ANG + HALF + g + 1, PAD : PAD + rows, 0:LANES].astype(F32)
                    x = roll(x, 16 * g + 2 + 64 * half)
                    a = x if a is None else jnp.where(group == g, x, a)
                    x = ext[si * ANG + HALF - g - 1, PAD : PAD + rows, cols - LANES : cols].astype(F32)
                    x = roll(x, 16 * g + 14 + 64 * half)
                    b = x if b is None else jnp.where(group == g, x, b)
            left = a if half == 0 else jnp.where(right_part, left, a)
            right = b if half == 0 else jnp.where(right_part, right, b)
        sp[0, slot] = left.astype(sp.dtype)
        sp[1, slot] = right.astype(sp.dtype)
    start(col_copies)

    center = [ext[CENTER, PAD : PAD + rows, h * LANES : (h + 1) * LANES].astype(F32) for h in range(2)]
    ca, cb = center
    for ti in range(ANG):
        move = D0 * (ti - HALF)
        ra, rb = roll(ca, move), roll(cb, move)
        if move > 0:
            cen[ti, 0] = ra
            cen[ti, 1] = jnp.where(lane >= move, rb, ra)
        elif move < 0:
            cen[ti, 0] = jnp.where(lane < LANES + move, ra, rb)
            cen[ti, 1] = rb
        else:
            cen[ti, 0] = ca
            cen[ti, 1] = cb
    total = jnp.zeros((rows, LANES), F32)
    for g in range(HALF):
        m = D0 * (g + 1)
        total = jnp.where(right_part & (group == g), roll(cb, 16 * g - 126 + m), total)
        total = jnp.where((~right_part) & (group == g), roll(ca, 78 + 16 * g - m), total)
    cpack[...] = total
    pacc[...] = jnp.zeros_like(pacc)

    chunk = 16
    clane = lane_of(chunk)

    def terms(v0, side, down, s, tscale, middle):
        slope = tscale * side if s == 0 else (0.5 * s) * down + tscale * side
        error = v0 - middle
        weighted = slope * lax.rsqrt(1.0 + error * error)
        return weighted * slope, weighted * error

    def view_pass(signs):
        def body(ti, carry):
            tscale = 0.5 * (ti - HALF).astype(F32)
            for slot, s in enumerate(signs):
                low = 0 if s < 0 else PAD
                size = rows if s == 0 else rows + PAD
                for h in range(2):
                    fb[slot, h, low : low + size, :] = ext[
                        ANG * (s + HALF) + ti, low : low + size, h * LANES : (h + 1) * LANES].astype(F32)
            for at in range(0, rows, chunk):
                sums = [[None, None], [None, None]]
                middle = [cen[ti, h, at : at + chunk, :] for h in range(2)]
                for slot, s in enumerate(signs):
                    base = PAD + D0 * s + at
                    v0 = [fb[slot, h, base : base + chunk, :] for h in range(2)]
                    after = [roll(v, -1) for v in v0]
                    before = [roll(v, 1) for v in v0]
                    after[0] = jnp.where(clane == LANES - 1, after[1], after[0])
                    before[1] = jnp.where(clane == 0, before[0], before[1])
                    for h in range(2):
                        down = None
                        if s:
                            down = fb[slot, h, base + 1 : base + 1 + chunk, :] - fb[slot, h, base - 1 : base - 1 + chunk, :]
                        data, src = terms(v0[h], after[h] - before[h], down, s, tscale, middle[h])
                        sums[0][h] = data if sums[0][h] is None else sums[0][h] + data
                        sums[1][h] = src if sums[1][h] is None else sums[1][h] + src
                for f in range(2):
                    for h in range(2):
                        old = sums[f][h] if signs == (0,) else acc[ti, f, h, at : at + chunk, :] + sums[f][h]
                        acc[ti, f, h, at : at + chunk, :] = old
            return carry

        lax.fori_loop(0, ANG, body, 0)

    view_pass((0,))
    for size in range(1, HALF + 1):
        arrive(row_copies[2 * size : 2 * size + 2])
        view_pass((size, -size))
    arrive(row_copies[:2] + col_copies)

    flane = lane_of(full)
    fgroup, fplace, fright = (flane % 64) // 16, flane % 16, flane < 64
    ptscale = jnp.where(clane < 64, 0.5, -0.5) * ((clane % 64) // 16 + 1).astype(F32)
    for si in range(ANG):
        s = si - HALF
        slot, half = ((0, 0), (0, 1), (1, 0), (1, 1), (2, 0), (3, 0), (3, 1), (4, 0), (4, 1))[si]
        low = 0 if s < 0 else PAD
        size = rows if s == 0 else rows + PAD
        part = slice(low, low + size)
        right, grp, plc = fright[part], fgroup[part], fplace[part]
        x, z = col_r[slot, part, :].astype(F32), col_l[slot, part, :].astype(F32)
        merged = jnp.where(right, roll(x, 64) if half else x, z if half else roll(z, 64))
        for g in range(HALF):
            a = ext[si * ANG + HALF - g - 1, part, 0:LANES].astype(F32)
            b = ext[si * ANG + HALF + g + 1, part, cols - LANES : cols].astype(F32)
            merged = jnp.where(right & (grp == g) & (plc < 2), roll(b, 16 * g + 2), merged)
            merged = jnp.where((~right) & (grp == g) & (plc >= 14), roll(a, 16 * g + 78), merged)
        pb[part, :] = merged
        for at in range(0, rows, chunk):
            base = PAD + D0 * s + at
            v0 = pb[base : base + chunk, :]
            down = pb[base + 1 : base + 1 + chunk, :] - pb[base - 1 : base - 1 + chunk, :] if s else None
            data, src = terms(v0, roll(v0, -1) - roll(v0, 1), down, s, ptscale, cpack[at : at + chunk, :])
            pacc[0, at : at + chunk, :] += data
            pacc[1, at : at + chunk, :] += src

    for f in range(2):
        ta, tb = acc[HALF, f, 0], acc[HALF, f, 1]
        for ti in range(ANG):
            m = D0 * abs(ti - HALF)
            if m == 0:
                continue
            a, b = acc[ti, f, 0], acc[ti, f, 1]
            g = m // D0 - 1
            if ti > HALF:
                ra, rb = roll(a, -m), roll(b, -m)
                ta = ta + jnp.where(lane < LANES - m, ra, rb)
                tb = tb + jnp.where(lane <= LANES - 2 - m, rb, roll(pacc[f], 126 - m - 16 * g))
            else:
                ra, rb = roll(a, m), roll(b, m)
                ta = ta + jnp.where(lane >= m + 1, ra, roll(pacc[f], m - 78 - 16 * g))
                tb = tb + jnp.where(lane >= m, rb, ra)
        own[f, :, 0:LANES] = ta
        own[f, :, LANES : 2 * LANES] = tb

    coeff = damping + own[0] * (1.0 / VIEWS)
    source = own[1] * (-1.0 / VIEWS)

    frows, fcols = rows + 16, cols + 2 * LANES
    bands = []
    for part in (slice(0, PAD), slice(PAD, PAD + rows), slice(PAD + rows, full)):
        bands.append(jnp.concatenate([
            col_l[2, part, :].astype(F32), ext[CENTER, part, :].astype(F32), roll(col_r[2, part, :].astype(F32), 64)], axis=1))
    cf = jnp.concatenate([bands[0][8:16], bands[1], bands[2][0:8]], axis=0)
    gcol = lax.broadcasted_iota(jnp.int32, (frows, fcols), 1) + (c * cols - LANES)
    grow = lax.broadcasted_iota(jnp.int32, (frows, fcols), 0) + (r * rows - 8)

    def east(x):
        return pltpu.roll(x, fcols - 1, 1)

    def west(x):
        return pltpu.roll(x, 1, 1)

    def south(x):
        return pltpu.roll(x, frows - 1, 0)

    def north(x):
        return pltpu.roll(x, 1, 0)

    dx = east(cf) - cf
    dy = south(cf) - cf
    edge_e = jnp.where((gcol >= 0) & (gcol < ncol * cols - 1), jnp.exp(-dx * dx), 0.0)
    edge_s = jnp.where((grow >= 0) & (grow < nrow * rows - 1), jnp.exp(-dy * dy), 0.0)
    edge_w, edge_n = west(edge_e), north(edge_s)
    weights = smooth_weight * (edge_e + edge_w + edge_s + edge_n)

    inner = (slice(8, 8 + rows), slice(LANES, LANES + cols))
    zed = source / (coeff + weights[inner])
    zc[0] = zed
    zc[1] = coeff
    gpack[0] = jnp.where(right_part, zed[:, 0:LANES], roll(coeff[:, 0:LANES], 64))
    gpack[1] = jnp.where(right_part, roll(coeff[:, cols - LANES : cols], 64), zed[:, cols - LANES : cols])

    copies2 = []
    for index, (dr, dc) in enumerate(DIRS):
        if dc == 0:
            src = zc.at[:, pl.ds(0, 8), :] if dr < 0 else zc.at[:, pl.ds(rows - 8, 8), :]
            dst = ghost_d if dr < 0 else ghost_u
        elif dr == 0:
            src = gpack.at[0] if dc < 0 else gpack.at[1]
            dst = ghost_r if dc < 0 else ghost_l
        else:
            src = gpack.at[0 if dc < 0 else 1, pl.ds(0 if dr < 0 else rows - 8, 8), :]
            dst = corner.at[index - 4]
        copies2.append((dr, dc, pltpu.make_async_remote_copy(
            src_ref=src, dst_ref=dst, send_sem=send2.at[index], recv_sem=recv2.at[index],
            device_id=(r + dr, c + dc), device_id_type=pl.DeviceIdType.MESH)))
    start(copies2)
    drain(row_copies + col_copies)
    arrive(copies2)

    zf = jnp.concatenate([
        jnp.concatenate([corner[3], ghost_u[0], corner[2]], axis=1),
        jnp.concatenate([ghost_l[...], zed, ghost_r[...]], axis=1),
        jnp.concatenate([corner[1], ghost_d[0], corner[0]], axis=1)], axis=0)
    one = jnp.ones((8, LANES), F32)
    kf = jnp.concatenate([
        jnp.concatenate([one, ghost_u[1], one], axis=1),
        jnp.concatenate([roll(ghost_l[...], 64), coeff, roll(ghost_r[...], 64)], axis=1),
        jnp.concatenate([one, ghost_d[1], one], axis=1)], axis=0)
    diag = kf + weights

    def operate(z):
        edges = edge_e * east(z) + edge_w * west(z) + edge_s * south(z) + edge_n * north(z)
        return diag * z - smooth_weight * edges

    wf = operate(zf)
    qf = wf / diag
    vf = operate(qf)
    w, q, v = wf[inner], qf[inner], vf[inner]
    rest = source - w
    y = zed - q
    wv = w - v
    sums = (zed * w, zed * rest, y * rest, q * rest, q * w, y * wv, y * v, q * v)
    line = lax.broadcasted_iota(jnp.int32, (1, LANES), 1)
    packed = jnp.zeros((1, LANES), F32)
    for i, x in enumerate(sums):
        x = jnp.sum(x, axis=0, keepdims=True)
        x = jnp.sum(x, axis=1, keepdims=True)
        packed = jnp.where(line == i, x, packed)
    redout[0] = packed
    redbuf[me] = packed

    def red_copy(i):
        peer = (me + i) % count
        return pltpu.make_async_remote_copy(
            src_ref=redout.at[0], dst_ref=redbuf.at[me], send_sem=rsend.at[0], recv_sem=rrecv.at[0],
            device_id=(peer // ncol, peer % ncol), device_id_type=pl.DeviceIdType.MESH)

    def cast_out(i, carry):
        red_copy(i).start()
        return carry

    lax.fori_loop(1, count, cast_out, 0)
    drain(copies2)
    others = redbuf.at[pl.ds(0, count - 1)]
    pltpu.make_async_copy(others, others, rrecv.at[0]).wait()
    pltpu.make_async_copy(others, others, rsend.at[0]).wait()
    totals = jnp.sum(redbuf[...], axis=0)
    b, e, f, g, h, k, l, m = [totals[:, i : i + 1] for i in range(8)]
    delta = e / b
    step0 = (e + b) / b
    rz0 = e + b
    rz1 = f - 2.0 * delta * g + delta * delta * h
    wu1 = k - 2.0 * delta * l + delta * delta * m
    beta = rz1 / rz0
    step1 = rz1 / (wu1 - beta * rz1 / step0)
    direction = (y - delta * q) + beta * zed
    image = (wv - delta * v) + beta * w
    inc[...] = step0 * zed + step1 * direction
    res[...] = (source - step0 * w) - step1 * image


def solution(mesh):
    nrow, ncol = mesh.shape["row"], mesh.shape["col"]

    def shards(views):
        _, rows, cols = views.shape
        full = PAD + rows + PAD
        bf = views.dtype
        return pl.pallas_call(
            functools.partial(kernel, nrow, ncol),
            out_shape=(jax.ShapeDtypeStruct((rows, cols), F32),) * 2,
            in_specs=[pl.BlockSpec(memory_space=pltpu.HBM)],
            out_specs=[pl.BlockSpec(memory_space=pltpu.VMEM)] * 2,
            scratch_shapes=[
                pltpu.VMEM((VIEWS, full, cols), bf),
                pltpu.VMEM((2, 5, rows, LANES), bf),
                pltpu.VMEM((5, full, LANES), bf),
                pltpu.VMEM((5, full, LANES), bf),
                pltpu.VMEM((2, 2, full, LANES), F32),
                pltpu.VMEM((full, LANES), F32),
                pltpu.VMEM((ANG, 2, rows, LANES), F32),
                pltpu.VMEM((rows, LANES), F32),
                pltpu.VMEM((ANG, 2, 2, rows, LANES), F32),
                pltpu.VMEM((2, rows, LANES), F32),
                pltpu.VMEM((2, rows, cols), F32),
                pltpu.VMEM((2, rows, cols), F32),
                pltpu.VMEM((2, rows, LANES), F32),
                pltpu.VMEM((2, 8, cols), F32),
                pltpu.VMEM((2, 8, cols), F32),
                pltpu.VMEM((rows, LANES), F32),
                pltpu.VMEM((rows, LANES), F32),
                pltpu.VMEM((4, 8, LANES), F32),
                pltpu.VMEM((nrow * ncol, 1, LANES), F32),
                pltpu.VMEM((1, 1, LANES), F32),
                pltpu.SemaphoreType.DMA((ANG,)),
                pltpu.SemaphoreType.DMA((16,)),
                pltpu.SemaphoreType.DMA((16,)),
                pltpu.SemaphoreType.DMA((8,)),
                pltpu.SemaphoreType.DMA((8,)),
                pltpu.SemaphoreType.DMA((1,)),
                pltpu.SemaphoreType.DMA((1,)),
            ],
            compiler_params=pltpu.CompilerParams(collective_id=0, has_side_effects=True, vmem_limit_bytes=48 << 20),
        )(views)

    return jax.shard_map(
        shards,
        mesh=mesh,
        in_specs=(P(None, "row", "col"),),
        out_specs=(P("row", "col"), P("row", "col")),
        check_vma=False,
    )
```

```python
import functools

import jax
import jax.numpy as jnp
from jax import lax
from jax.experimental import pallas as pl
from jax.experimental.pallas import tpu as pltpu
from jax.sharding import PartitionSpec as P

ANG = 9
VIEWS = 81
HALF = 4
CENTER = 40
D0 = 3
smooth_weight = 2.0
damping = 0.1
PAD = 16
LANES = 128
F32 = jnp.float32
DIRS = ((-1, 0), (1, 0), (0, -1), (0, 1), (-1, -1), (-1, 1), (1, -1), (1, 1))


def roll(x, shift):
    return pltpu.roll(x, shift % LANES, 1)


def lane_of(rows):
    return lax.broadcasted_iota(jnp.int32, (rows, LANES), 1)


def kernel(nrow, ncol, views, out, ext, sp, col_r, col_l, fb, pb, cen, cpack, acc, pacc, own, zc, gpack,
           ghost_u, ghost_d, ghost_l, ghost_r, corner, redbuf, redout, load_sem, send1, recv1, send2, recv2, rsend, rrecv):
    rows, cols = views.shape[1], views.shape[2]
    r, c = lax.axis_index("row"), lax.axis_index("col")
    count = nrow * ncol
    me = r * ncol + c
    full = PAD + rows + PAD

    def exists(dr, dc):
        return (r + dr >= 0) & (r + dr < nrow) & (c + dc >= 0) & (c + dc < ncol)

    barrier = pltpu.get_barrier_semaphore()

    def greet(i, carry):
        peer = (me + i) % count
        pl.semaphore_signal(barrier, inc=1, device_id=(peer // ncol, peer % ncol), device_id_type=pl.DeviceIdType.MESH)
        return carry

    lax.fori_loop(1, count, greet, 0)

    loads = []
    for si in range(ANG):
        part = pl.ds(si * ANG, ANG)
        copy = pltpu.make_async_copy(views.at[part], ext.at[part, pl.ds(PAD, rows), :], load_sem.at[si])
        copy.start()
        loads.append(copy)

    def zero(ref, first, number, row, size):
        def body(i, carry):
            ref[first + i, row : row + size, :] = jnp.zeros((size, ref.shape[2]), ref.dtype)
            return carry
        lax.fori_loop(0, number, body, 0)

    @pl.when(r == 0)
    def _():
        zero(ext, 0, 41, 0, PAD)

    @pl.when(r == nrow - 1)
    def _():
        zero(ext, 40, 41, PAD + rows, PAD)

    for ref, edge in ((col_r, c == ncol - 1), (col_l, c == 0)):
        @pl.when(edge)
        def _():
            zero(ref, 0, 5, PAD, rows)

        @pl.when(edge | (r == 0))
        def _():
            zero(ref, 0, 3, 0, PAD)

        @pl.when(edge | (r == nrow - 1))
        def _():
            zero(ref, 2, 3, PAD + rows, PAD)

    for edge, ref in ((r == 0, ghost_u), (r == nrow - 1, ghost_d)):
        @pl.when(edge)
        def _():
            ref[0] = jnp.zeros((8, cols), F32)
            ref[1] = jnp.ones((8, cols), F32)
    for edge, ref, low in ((c == 0, ghost_l, 1.0), (c == ncol - 1, ghost_r, 0.0)):
        @pl.when(edge)
        def _():
            ref[...] = jnp.where(lane_of(rows) < 64, low, 1.0 - low)
    for index, (dr, dc) in enumerate(DIRS[4:]):
        @pl.when(jnp.logical_not(exists(-dr, -dc)))
        def _():
            corner[index] = jnp.zeros((8, LANES), F32)


    row_copies = []
    for size in range(HALF + 1):
        reach = 8 if D0 * size + 1 <= 8 else PAD
        for index, (dr, dc) in enumerate(DIRS[:2]):
            if size == 0:
                part = pl.ds(CENTER, 1)
            else:
                part = pl.ds(ANG * (HALF - dr * size), ANG)
            if dr < 0:
                src, dst = views.at[part, pl.ds(0, reach), :], ext.at[part, pl.ds(PAD + rows, reach), :]
            else:
                src, dst = views.at[part, pl.ds(rows - reach, reach), :], ext.at[part, pl.ds(PAD - reach, reach), :]
            row_copies.append((dr, dc, pltpu.make_async_remote_copy(
                src_ref=src, dst_ref=dst, send_sem=send1.at[2 * size + index], recv_sem=recv1.at[2 * size + index],
                device_id=(r + dr, c + dc), device_id_type=pl.DeviceIdType.MESH)))
    col_copies = []
    for index, (dr, dc) in enumerate(DIRS[2:]):
        side = col_r if dc < 0 else col_l
        mine = sp.at[0 if dc < 0 else 1]
        if dr == 0:
            src, dst = mine, side.at[:, pl.ds(PAD, rows), :]
        elif dr < 0:
            src, dst = mine.at[pl.ds(2, 3), pl.ds(0, PAD), :], side.at[pl.ds(2, 3), pl.ds(PAD + rows, PAD), :]
        else:
            src, dst = mine.at[pl.ds(0, 3), pl.ds(rows - PAD, PAD), :], side.at[pl.ds(0, 3), pl.ds(0, PAD), :]
        col_copies.append((dr, dc, pltpu.make_async_remote_copy(
            src_ref=src, dst_ref=dst, send_sem=send1.at[10 + index], recv_sem=recv1.at[10 + index],
            device_id=(r + dr, c + dc), device_id_type=pl.DeviceIdType.MESH)))

    def start(group):
        for dr, dc, copy in group:
            @pl.when(exists(dr, dc))
            def _():
                copy.start()

    def arrive(group):
        for dr, dc, copy in group:
            @pl.when(exists(-dr, -dc))
            def _():
                copy.wait_recv()

    def drain(group):
        for dr, dc, copy in group:
            @pl.when(exists(dr, dc))
            def _():
                copy.wait_send()

    for copy in loads:
        copy.wait()

    lane = lane_of(rows)
    group = (lane % 64) // 16
    place = lane % 16
    right_part = lane < 64

    for slot in range(5):
        left = right = None
        for half in range(2):
            if slot == 2 and half == 1:
                a = roll(ext[CENTER, PAD : PAD + rows, 0:LANES].astype(F32), 64)
                b = ext[CENTER, PAD : PAD + rows, cols - LANES : cols].astype(F32)
            else:
                si = (0, 2, 4, 5, 7)[slot] + half
                a = b = None
                for g in range(HALF):
                    x = ext[si * ANG + HALF + g + 1, PAD : PAD + rows, 0:LANES].astype(F32)
                    x = roll(x, 16 * g + 2 + 64 * half)
                    a = x if a is None else jnp.where(group == g, x, a)
                    x = ext[si * ANG + HALF - g - 1, PAD : PAD + rows, cols - LANES : cols].astype(F32)
                    x = roll(x, 16 * g + 14 + 64 * half)
                    b = x if b is None else jnp.where(group == g, x, b)
            left = a if half == 0 else jnp.where(right_part, left, a)
            right = b if half == 0 else jnp.where(right_part, right, b)
        sp[0, slot] = left.astype(sp.dtype)
        sp[1, slot] = right.astype(sp.dtype)
    pl.semaphore_wait(barrier, count - 1)
    start(row_copies)
    start(col_copies)

    center = [ext[CENTER, PAD : PAD + rows, h * LANES : (h + 1) * LANES].astype(F32) for h in range(2)]
    ca, cb = center
    for ti in range(ANG):
        move = D0 * (ti - HALF)
        ra, rb = roll(ca, move), roll(cb, move)
        if move > 0:
            cen[ti, 0] = ra
            cen[ti, 1] = jnp.where(lane >= move, rb, ra)
        elif move < 0:
            cen[ti, 0] = jnp.where(lane < LANES + move, ra, rb)
            cen[ti, 1] = rb
        else:
            cen[ti, 0] = ca
            cen[ti, 1] = cb
    total = jnp.zeros((rows, LANES), F32)
    for g in range(HALF):
        m = D0 * (g + 1)
        total = jnp.where(right_part & (group == g), roll(cb, 16 * g - 126 + m), total)
        total = jnp.where((~right_part) & (group == g), roll(ca, 78 + 16 * g - m), total)
    cpack[...] = total
    pacc[...] = jnp.zeros_like(pacc)

    chunk = 16
    clane = lane_of(chunk)

    def terms(v0, side, down, s, tscale, middle):
        slope = tscale * side if s == 0 else (0.5 * s) * down + tscale * side
        error = v0 - middle
        weighted = slope * lax.rsqrt(1.0 + error * error)
        return weighted * slope, weighted * error

    def view_step(ti, tscale, slot, s, at, middle, sums):
        base = PAD + D0 * s + at
        v0 = [fb[slot, h, base : base + chunk, :] for h in range(2)]
        after = [roll(v, -1) for v in v0]
        before = [roll(v, 1) for v in v0]
        after[0] = jnp.where(clane == LANES - 1, after[1], after[0])
        before[1] = jnp.where(clane == 0, before[0], before[1])
        for h in range(2):
            down = None
            if s:
                down = fb[slot, h, base + 1 : base + 1 + chunk, :] - fb[slot, h, base - 1 : base - 1 + chunk, :]
            data, src = terms(v0[h], after[h] - before[h], down, s, tscale, middle[h])
            sums[0][h] = data if sums[0][h] is None else sums[0][h] + data
            sums[1][h] = src if sums[1][h] is None else sums[1][h] + src

    def widen(ti, slot, s, low, high):
        for h in range(2):
            fb[slot, h, low:high, :] = ext[ANG * (s + HALF) + ti, low:high, h * LANES : (h + 1) * LANES].astype(F32)

    def view_pass(signs):
        def body(ti, carry):
            tscale = 0.5 * (ti - HALF).astype(F32)
            for slot, s in enumerate(signs):
                widen(ti, slot, s, PAD, PAD + rows)
            for at in range(0, rows, chunk):
                sums = [[None, None], [None, None]]
                middle = [cen[ti, h, at : at + chunk, :] for h in range(2)]
                for slot, s in enumerate(signs):
                    if not ((s > 0 and at == rows - chunk) or (s < 0 and at == 0)):
                        view_step(ti, tscale, slot, s, at, middle, sums)
                for f in range(2):
                    for h in range(2):
                        old = sums[f][h] if signs == (0,) else acc[ti, f, h, at : at + chunk, :] + sums[f][h]
                        acc[ti, f, h, at : at + chunk, :] = old
            return carry

        lax.fori_loop(0, ANG, body, 0)

    view_pass((0,))
    for size in range(1, HALF + 1):
        view_pass((size, -size))
    arrive(row_copies)

    def edge_pass(ti, carry):
        tscale = 0.5 * (ti - HALF).astype(F32)
        for sign, at in ((1, rows - chunk), (-1, 0)):
            sums = [[acc[ti, f, h, at : at + chunk, :] for h in range(2)] for f in range(2)]
            middle = [cen[ti, h, at : at + chunk, :] for h in range(2)]
            for size in range(1, HALF + 1):
                slot = 2 * (size - 1) + (sign < 0)
                low = PAD + at if sign > 0 else 0
                widen(ti, slot, sign * size, low, low + 2 * PAD)
                view_step(ti, tscale, slot, sign * size, at, middle, sums)
            for f in range(2):
                for h in range(2):
                    acc[ti, f, h, at : at + chunk, :] = sums[f][h]
        return carry

    lax.fori_loop(0, ANG, edge_pass, 0)
    arrive(col_copies)

    flane = lane_of(full)
    fgroup, fplace, fright = (flane % 64) // 16, flane % 16, flane < 64
    ptscale = jnp.where(clane < 64, 0.5, -0.5) * ((clane % 64) // 16 + 1).astype(F32)
    for si in range(ANG):
        s = si - HALF
        slot, half = ((0, 0), (0, 1), (1, 0), (1, 1), (2, 0), (3, 0), (3, 1), (4, 0), (4, 1))[si]
        low = 0 if s < 0 else PAD
        size = rows if s == 0 else rows + PAD
        part = slice(low, low + size)
        right, grp, plc = fright[part], fgroup[part], fplace[part]
        x, z = col_r[slot, part, :].astype(F32), col_l[slot, part, :].astype(F32)
        merged = jnp.where(right, roll(x, 64) if half else x, z if half else roll(z, 64))
        for g in range(HALF):
            a = ext[si * ANG + HALF - g - 1, part, 0:LANES].astype(F32)
            b = ext[si * ANG + HALF + g + 1, part, cols - LANES : cols].astype(F32)
            merged = jnp.where(right & (grp == g) & (plc < 2), roll(b, 16 * g + 2), merged)
            merged = jnp.where((~right) & (grp == g) & (plc >= 14), roll(a, 16 * g + 78), merged)
        pb[part, :] = merged
        for at in range(0, rows, chunk):
            base = PAD + D0 * s + at
            v0 = pb[base : base + chunk, :]
            down = pb[base + 1 : base + 1 + chunk, :] - pb[base - 1 : base - 1 + chunk, :] if s else None
            data, src = terms(v0, roll(v0, -1) - roll(v0, 1), down, s, ptscale, cpack[at : at + chunk, :])
            pacc[0, at : at + chunk, :] += data
            pacc[1, at : at + chunk, :] += src

    for f in range(2):
        ta, tb = acc[HALF, f, 0], acc[HALF, f, 1]
        for ti in range(ANG):
            m = D0 * abs(ti - HALF)
            if m == 0:
                continue
            a, b = acc[ti, f, 0], acc[ti, f, 1]
            g = m // D0 - 1
            if ti > HALF:
                ra, rb = roll(a, -m), roll(b, -m)
                ta = ta + jnp.where(lane < LANES - m, ra, rb)
                tb = tb + jnp.where(lane <= LANES - 2 - m, rb, roll(pacc[f], 126 - m - 16 * g))
            else:
                ra, rb = roll(a, m), roll(b, m)
                ta = ta + jnp.where(lane >= m + 1, ra, roll(pacc[f], m - 78 - 16 * g))
                tb = tb + jnp.where(lane >= m, rb, ra)
        own[f, :, 0:LANES] = ta
        own[f, :, LANES : 2 * LANES] = tb

    coeff = damping + own[0] * (1.0 / VIEWS)
    source = own[1] * (-1.0 / VIEWS)

    frows, fcols = rows + 16, cols + 2 * LANES
    bands = []
    for part in (slice(0, PAD), slice(PAD, PAD + rows), slice(PAD + rows, full)):
        bands.append(jnp.concatenate([
            col_l[2, part, :].astype(F32), ext[CENTER, part, :].astype(F32), roll(col_r[2, part, :].astype(F32), 64)], axis=1))
    cf = jnp.concatenate([bands[0][8:16], bands[1], bands[2][0:8]], axis=0)
    gcol = lax.broadcasted_iota(jnp.int32, (frows, fcols), 1) + (c * cols - LANES)
    grow = lax.broadcasted_iota(jnp.int32, (frows, fcols), 0) + (r * rows - 8)

    def east(x):
        return pltpu.roll(x, fcols - 1, 1)

    def west(x):
        return pltpu.roll(x, 1, 1)

    def south(x):
        return pltpu.roll(x, frows - 1, 0)

    def north(x):
        return pltpu.roll(x, 1, 0)

    dx = east(cf) - cf
    dy = south(cf) - cf
    edge_e = jnp.where((gcol >= 0) & (gcol < ncol * cols - 1), jnp.exp(-dx * dx), 0.0)
    edge_s = jnp.where((grow >= 0) & (grow < nrow * rows - 1), jnp.exp(-dy * dy), 0.0)
    edge_w, edge_n = west(edge_e), north(edge_s)
    weights = smooth_weight * (edge_e + edge_w + edge_s + edge_n)

    inner = (slice(8, 8 + rows), slice(LANES, LANES + cols))
    zed = source / (coeff + weights[inner])
    zc[0] = zed
    zc[1] = coeff
    gpack[0] = jnp.where(right_part, zed[:, 0:LANES], roll(coeff[:, 0:LANES], 64))
    gpack[1] = jnp.where(right_part, roll(coeff[:, cols - LANES : cols], 64), zed[:, cols - LANES : cols])

    copies2 = []
    for index, (dr, dc) in enumerate(DIRS):
        if dc == 0:
            src = zc.at[:, pl.ds(0, 8), :] if dr < 0 else zc.at[:, pl.ds(rows - 8, 8), :]
            dst = ghost_d if dr < 0 else ghost_u
        elif dr == 0:
            src = gpack.at[0] if dc < 0 else gpack.at[1]
            dst = ghost_r if dc < 0 else ghost_l
        else:
            src = gpack.at[0 if dc < 0 else 1, pl.ds(0 if dr < 0 else rows - 8, 8), :]
            dst = corner.at[index - 4]
        copies2.append((dr, dc, pltpu.make_async_remote_copy(
            src_ref=src, dst_ref=dst, send_sem=send2.at[index], recv_sem=recv2.at[index],
            device_id=(r + dr, c + dc), device_id_type=pl.DeviceIdType.MESH)))
    start(copies2)
    drain(row_copies + col_copies)
    arrive(copies2)

    zf = jnp.concatenate([
        jnp.concatenate([corner[3], ghost_u[0], corner[2]], axis=1),
        jnp.concatenate([ghost_l[...], zed, ghost_r[...]], axis=1),
        jnp.concatenate([corner[1], ghost_d[0], corner[0]], axis=1)], axis=0)
    one = jnp.ones((8, LANES), F32)
    kf = jnp.concatenate([
        jnp.concatenate([one, ghost_u[1], one], axis=1),
        jnp.concatenate([roll(ghost_l[...], 64), coeff, roll(ghost_r[...], 64)], axis=1),
        jnp.concatenate([one, ghost_d[1], one], axis=1)], axis=0)
    diag = kf + weights

    def operate(z):
        edges = edge_e * east(z) + edge_w * west(z) + edge_s * south(z) + edge_n * north(z)
        return diag * z - smooth_weight * edges

    wf = operate(zf)
    qf = wf / diag
    vf = operate(qf)
    w, q, v = wf[inner], qf[inner], vf[inner]
    rest = source - w
    y = zed - q
    wv = w - v
    sums = (zed * w, zed * rest, y * rest, q * rest, q * w, y * wv, y * v, q * v)
    line = lax.broadcasted_iota(jnp.int32, (1, LANES), 1)
    packed = jnp.zeros((1, LANES), F32)
    for i, x in enumerate(sums):
        x = jnp.sum(x, axis=0, keepdims=True)
        x = jnp.sum(x, axis=1, keepdims=True)
        packed = jnp.where(line == i, x, packed)
    redout[0] = packed
    redbuf[me] = packed

    def red_copy(i):
        peer = (me + i) % count
        return pltpu.make_async_remote_copy(
            src_ref=redout.at[0], dst_ref=redbuf.at[me], send_sem=rsend.at[0], recv_sem=rrecv.at[0],
            device_id=(peer // ncol, peer % ncol), device_id_type=pl.DeviceIdType.MESH)

    def cast_out(i, carry):
        red_copy(i).start()
        return carry

    lax.fori_loop(1, count, cast_out, 0)
    drain(copies2)
    others = redbuf.at[pl.ds(0, count - 1)]
    pltpu.make_async_copy(others, others, rrecv.at[0]).wait()
    pltpu.make_async_copy(others, others, rsend.at[0]).wait()
    totals = jnp.sum(redbuf[...], axis=0)
    b, e, f, g, h, k, l, m = [totals[:, i : i + 1] for i in range(8)]
    delta = e / b
    step0 = (e + b) / b
    rz0 = e + b
    rz1 = f - 2.0 * delta * g + delta * delta * h
    wu1 = k - 2.0 * delta * l + delta * delta * m
    beta = rz1 / rz0
    step1 = rz1 / (wu1 - beta * rz1 / step0)
    direction = (y - delta * q) + beta * zed
    image = (wv - delta * v) + beta * w
    out[0] = step0 * zed + step1 * direction
    out[1] = (source - step0 * w) - step1 * image


def solution(mesh):
    nrow, ncol = mesh.shape["row"], mesh.shape["col"]

    def shards(views):
        _, rows, cols = views.shape
        full = PAD + rows + PAD
        bf = views.dtype
        out = pl.pallas_call(
            functools.partial(kernel, nrow, ncol),
            out_shape=jax.ShapeDtypeStruct((2, rows, cols), F32),
            in_specs=[pl.BlockSpec(memory_space=pltpu.HBM)],
            out_specs=pl.BlockSpec(memory_space=pltpu.VMEM),
            scratch_shapes=[
                pltpu.VMEM((VIEWS, full, cols), bf),
                pltpu.VMEM((2, 5, rows, LANES), bf),
                pltpu.VMEM((5, full, LANES), bf),
                pltpu.VMEM((5, full, LANES), bf),
                pltpu.VMEM((8, 2, full, LANES), F32),
                pltpu.VMEM((full, LANES), F32),
                pltpu.VMEM((ANG, 2, rows, LANES), F32),
                pltpu.VMEM((rows, LANES), F32),
                pltpu.VMEM((ANG, 2, 2, rows, LANES), F32),
                pltpu.VMEM((2, rows, LANES), F32),
                pltpu.VMEM((2, rows, cols), F32),
                pltpu.VMEM((2, rows, cols), F32),
                pltpu.VMEM((2, rows, LANES), F32),
                pltpu.VMEM((2, 8, cols), F32),
                pltpu.VMEM((2, 8, cols), F32),
                pltpu.VMEM((rows, LANES), F32),
                pltpu.VMEM((rows, LANES), F32),
                pltpu.VMEM((4, 8, LANES), F32),
                pltpu.VMEM((nrow * ncol, 1, LANES), F32),
                pltpu.VMEM((1, 1, LANES), F32),
                pltpu.SemaphoreType.DMA((ANG,)),
                pltpu.SemaphoreType.DMA((16,)),
                pltpu.SemaphoreType.DMA((16,)),
                pltpu.SemaphoreType.DMA((8,)),
                pltpu.SemaphoreType.DMA((8,)),
                pltpu.SemaphoreType.DMA((1,)),
                pltpu.SemaphoreType.DMA((1,)),
            ],
            compiler_params=pltpu.CompilerParams(collective_id=0, has_side_effects=True, vmem_limit_bytes=48 << 20),
        )(pltpu.with_memory_space_constraint(views, pltpu.HBM))
        return out[0], out[1]

    return jax.shard_map(
        shards,
        mesh=mesh,
        in_specs=(P(None, "row", "col"),),
        out_specs=(P("row", "col"), P("row", "col")),
        check_vma=False,
    )
```

```python
import functools

import jax
import jax.numpy as jnp
from jax import lax
from jax.experimental import pallas as pl
from jax.experimental.pallas import tpu as pltpu
from jax.sharding import PartitionSpec as P

ANG = 9
VIEWS = 81
HALF = 4
CENTER = 40
D0 = 3
smooth_weight = 2.0
damping = 0.1
PAD = 16
LANES = 128
F32 = jnp.float32
DIRS = ((-1, 0), (1, 0), (0, -1), (0, 1), (-1, -1), (-1, 1), (1, -1), (1, 1))


def roll(x, shift):
    return pltpu.roll(x, shift % LANES, 1)


def lane_of(rows):
    return lax.broadcasted_iota(jnp.int32, (rows, LANES), 1)


def kernel(nrow, ncol, views, out, ext, sp, col_r, col_l, fb, pb, cen, cpack, acc, pacc, own, zc, gpack,
           ghost_u, ghost_d, ghost_l, ghost_r, corner, redbuf, redout, load_sem, send1, recv1, send2, recv2, rsend, rrecv):
    rows, cols = views.shape[1], views.shape[2]
    r, c = lax.axis_index("row"), lax.axis_index("col")
    count = nrow * ncol
    me = r * ncol + c
    full = PAD + rows + PAD

    def exists(dr, dc):
        return (r + dr >= 0) & (r + dr < nrow) & (c + dc >= 0) & (c + dc < ncol)

    barrier = pltpu.get_barrier_semaphore()

    def greet(i, carry):
        peer = (me + i) % count
        pl.semaphore_signal(barrier, inc=1, device_id=(peer // ncol, peer % ncol), device_id_type=pl.DeviceIdType.MESH)
        return carry

    lax.fori_loop(1, count, greet, 0)

    loads = []
    for si in range(ANG):
        part = pl.ds(si * ANG, ANG)
        copy = pltpu.make_async_copy(views.at[part], ext.at[part, pl.ds(PAD, rows), :], load_sem.at[si])
        copy.start()
        loads.append(copy)

    def zero(ref, first, number, row, size):
        def body(i, carry):
            ref[first + i, row : row + size, :] = jnp.zeros((size, ref.shape[2]), ref.dtype)
            return carry
        lax.fori_loop(0, number, body, 0)

    @pl.when(r == 0)
    def _():
        zero(ext, 0, 41, 0, PAD)

    @pl.when(r == nrow - 1)
    def _():
        zero(ext, 40, 41, PAD + rows, PAD)

    for ref, edge in ((col_r, c == ncol - 1), (col_l, c == 0)):
        @pl.when(edge)
        def _():
            zero(ref, 0, 5, PAD, rows)

        @pl.when(edge | (r == 0))
        def _():
            zero(ref, 0, 3, 0, PAD)

        @pl.when(edge | (r == nrow - 1))
        def _():
            zero(ref, 2, 3, PAD + rows, PAD)

    for edge, ref in ((r == 0, ghost_u), (r == nrow - 1, ghost_d)):
        @pl.when(edge)
        def _():
            ref[0] = jnp.zeros((8, cols), F32)
            ref[1] = jnp.ones((8, cols), F32)
    for edge, ref, low in ((c == 0, ghost_l, 1.0), (c == ncol - 1, ghost_r, 0.0)):
        @pl.when(edge)
        def _():
            ref[...] = jnp.where(lane_of(rows) < 64, low, 1.0 - low)
    for index, (dr, dc) in enumerate(DIRS[4:]):
        @pl.when(jnp.logical_not(exists(-dr, -dc)))
        def _():
            corner[index] = jnp.zeros((8, LANES), F32)


    row_copies = []
    for size in range(HALF + 1):
        reach = 8 if D0 * size + 1 <= 8 else PAD
        for index, (dr, dc) in enumerate(DIRS[:2]):
            if size == 0:
                part = pl.ds(CENTER, 1)
            else:
                part = pl.ds(ANG * (HALF - dr * size), ANG)
            if dr < 0:
                src, dst = views.at[part, pl.ds(0, reach), :], ext.at[part, pl.ds(PAD + rows, reach), :]
            else:
                src, dst = views.at[part, pl.ds(rows - reach, reach), :], ext.at[part, pl.ds(PAD - reach, reach), :]
            row_copies.append((dr, dc, pltpu.make_async_remote_copy(
                src_ref=src, dst_ref=dst, send_sem=send1.at[2 * size + index], recv_sem=recv1.at[2 * size + index],
                device_id=(r + dr, c + dc), device_id_type=pl.DeviceIdType.MESH)))
    col_copies = []
    for index, (dr, dc) in enumerate(DIRS[2:]):
        side = col_r if dc < 0 else col_l
        mine = sp.at[0 if dc < 0 else 1]
        if dr == 0:
            src, dst = mine, side.at[:, pl.ds(PAD, rows), :]
        elif dr < 0:
            src, dst = mine.at[pl.ds(2, 3), pl.ds(0, PAD), :], side.at[pl.ds(2, 3), pl.ds(PAD + rows, PAD), :]
        else:
            src, dst = mine.at[pl.ds(0, 3), pl.ds(rows - PAD, PAD), :], side.at[pl.ds(0, 3), pl.ds(0, PAD), :]
        col_copies.append((dr, dc, pltpu.make_async_remote_copy(
            src_ref=src, dst_ref=dst, send_sem=send1.at[10 + index], recv_sem=recv1.at[10 + index],
            device_id=(r + dr, c + dc), device_id_type=pl.DeviceIdType.MESH)))

    def start(group):
        for dr, dc, copy in group:
            @pl.when(exists(dr, dc))
            def _():
                copy.start()

    def arrive(group):
        for dr, dc, copy in group:
            @pl.when(exists(-dr, -dc))
            def _():
                copy.wait_recv()

    def drain(group):
        for dr, dc, copy in group:
            @pl.when(exists(dr, dc))
            def _():
                copy.wait_send()

    pl.semaphore_wait(barrier, count - 1)
    start(row_copies)
    for copy in loads:
        copy.wait()

    lane = lane_of(rows)
    group = (lane % 64) // 16
    place = lane % 16
    right_part = lane < 64

    for slot in range(5):
        left = right = None
        for half in range(2):
            if slot == 2 and half == 1:
                a = roll(ext[CENTER, PAD : PAD + rows, 0:LANES].astype(F32), 64)
                b = ext[CENTER, PAD : PAD + rows, cols - LANES : cols].astype(F32)
            else:
                si = (0, 2, 4, 5, 7)[slot] + half
                a = b = None
                for g in range(HALF):
                    x = ext[si * ANG + HALF + g + 1, PAD : PAD + rows, 0:LANES].astype(F32)
                    x = roll(x, 16 * g + 2 + 64 * half)
                    a = x if a is None else jnp.where(group == g, x, a)
                    x = ext[si * ANG + HALF - g - 1, PAD : PAD + rows, cols - LANES : cols].astype(F32)
                    x = roll(x, 16 * g + 14 + 64 * half)
                    b = x if b is None else jnp.where(group == g, x, b)
            left = a if half == 0 else jnp.where(right_part, left, a)
            right = b if half == 0 else jnp.where(right_part, right, b)
        sp[0, slot] = left.astype(sp.dtype)
        sp[1, slot] = right.astype(sp.dtype)
    start(col_copies)

    center = [ext[CENTER, PAD : PAD + rows, h * LANES : (h + 1) * LANES].astype(F32) for h in range(2)]
    ca, cb = center
    for ti in range(ANG):
        move = D0 * (ti - HALF)
        ra, rb = roll(ca, move), roll(cb, move)
        if move > 0:
            cen[ti, 0] = ra
            cen[ti, 1] = jnp.where(lane >= move, rb, ra)
        elif move < 0:
            cen[ti, 0] = jnp.where(lane < LANES + move, ra, rb)
            cen[ti, 1] = rb
        else:
            cen[ti, 0] = ca
            cen[ti, 1] = cb
    total = jnp.zeros((rows, LANES), F32)
    for g in range(HALF):
        m = D0 * (g + 1)
        total = jnp.where(right_part & (group == g), roll(cb, 16 * g - 126 + m), total)
        total = jnp.where((~right_part) & (group == g), roll(ca, 78 + 16 * g - m), total)
    cpack[...] = total
    pacc[...] = jnp.zeros_like(pacc)

    chunk = 16
    clane = lane_of(chunk)

    def terms(v0, side, down, s, tscale, middle):
        slope = tscale * side if s == 0 else (0.5 * s) * down + tscale * side
        error = v0 - middle
        weighted = slope * lax.rsqrt(1.0 + error * error)
        return weighted * slope, weighted * error

    def view_step(ti, tscale, slot, s, at, middle, sums):
        base = PAD + D0 * s + at
        v0 = [fb[slot, h, base : base + chunk, :] for h in range(2)]
        after = [roll(v, -1) for v in v0]
        before = [roll(v, 1) for v in v0]
        after[0] = jnp.where(clane == LANES - 1, after[1], after[0])
        before[1] = jnp.where(clane == 0, before[0], before[1])
        for h in range(2):
            down = None
            if s:
                down = fb[slot, h, base + 1 : base + 1 + chunk, :] - fb[slot, h, base - 1 : base - 1 + chunk, :]
            data, src = terms(v0[h], after[h] - before[h], down, s, tscale, middle[h])
            sums[0][h] = data if sums[0][h] is None else sums[0][h] + data
            sums[1][h] = src if sums[1][h] is None else sums[1][h] + src

    def widen(ti, slot, s, low, high):
        for h in range(2):
            fb[slot, h, low:high, :] = ext[ANG * (s + HALF) + ti, low:high, h * LANES : (h + 1) * LANES].astype(F32)

    def view_pass(signs):
        def body(ti, carry):
            tscale = 0.5 * (ti - HALF).astype(F32)
            for slot, s in enumerate(signs):
                widen(ti, slot, s, PAD, PAD + rows)
            for at in range(0, rows, chunk):
                sums = [[None, None], [None, None]]
                middle = [cen[ti, h, at : at + chunk, :] for h in range(2)]
                for slot, s in enumerate(signs):
                    if not ((s > 0 and at == rows - chunk) or (s < 0 and at == 0)):
                        view_step(ti, tscale, slot, s, at, middle, sums)
                for f in range(2):
                    for h in range(2):
                        old = sums[f][h] if signs == (0,) else acc[ti, f, h, at : at + chunk, :] + sums[f][h]
                        acc[ti, f, h, at : at + chunk, :] = old
            return carry

        lax.fori_loop(0, ANG, body, 0)

    view_pass((0,))
    for size in range(1, HALF + 1):
        view_pass((size, -size))
    arrive(row_copies[:2] + col_copies)
    frows, fcols = rows + 16, cols + 2 * LANES
    bands = []
    for part in (slice(0, PAD), slice(PAD, PAD + rows), slice(PAD + rows, full)):
        bands.append(jnp.concatenate([
            col_l[2, part, :].astype(F32), ext[CENTER, part, :].astype(F32), roll(col_r[2, part, :].astype(F32), 64)], axis=1))
    cf = jnp.concatenate([bands[0][8:16], bands[1], bands[2][0:8]], axis=0)
    gcol = lax.broadcasted_iota(jnp.int32, (frows, fcols), 1) + (c * cols - LANES)
    grow = lax.broadcasted_iota(jnp.int32, (frows, fcols), 0) + (r * rows - 8)

    def east(x):
        return pltpu.roll(x, fcols - 1, 1)

    def west(x):
        return pltpu.roll(x, 1, 1)

    def south(x):
        return pltpu.roll(x, frows - 1, 0)

    def north(x):
        return pltpu.roll(x, 1, 0)

    dx = east(cf) - cf
    dy = south(cf) - cf
    edge_e = jnp.where((gcol >= 0) & (gcol < ncol * cols - 1), jnp.exp(-dx * dx), 0.0)
    edge_s = jnp.where((grow >= 0) & (grow < nrow * rows - 1), jnp.exp(-dy * dy), 0.0)
    edge_w, edge_n = west(edge_e), north(edge_s)
    weights = smooth_weight * (edge_e + edge_w + edge_s + edge_n)

    flane = lane_of(full)
    fgroup, fplace, fright = (flane % 64) // 16, flane % 16, flane < 64
    ptscale = jnp.where(clane < 64, 0.5, -0.5) * ((clane % 64) // 16 + 1).astype(F32)

    def packed_rows(si, low, high):
        slot, half = ((0, 0), (0, 1), (1, 0), (1, 1), (2, 0), (3, 0), (3, 1), (4, 0), (4, 1))[si]
        part = slice(low, high)
        right, grp, plc = fright[part], fgroup[part], fplace[part]
        x, z = col_r[slot, part, :].astype(F32), col_l[slot, part, :].astype(F32)
        merged = jnp.where(right, roll(x, 64) if half else x, z if half else roll(z, 64))
        for g in range(HALF):
            a = ext[si * ANG + HALF - g - 1, part, 0:LANES].astype(F32)
            b = ext[si * ANG + HALF + g + 1, part, cols - LANES : cols].astype(F32)
            merged = jnp.where(right & (grp == g) & (plc < 2), roll(b, 16 * g + 2), merged)
            merged = jnp.where((~right) & (grp == g) & (plc >= 14), roll(a, 16 * g + 78), merged)
        pb[si, part, :] = merged

    def packed_step(si, at):
        s = si - HALF
        base = PAD + D0 * s + at
        v0 = pb[si, base : base + chunk, :]
        down = pb[si, base + 1 : base + 1 + chunk, :] - pb[si, base - 1 : base - 1 + chunk, :] if s else None
        data, src = terms(v0, roll(v0, -1) - roll(v0, 1), down, s, ptscale, cpack[at : at + chunk, :])
        pacc[0, at : at + chunk, :] += data
        pacc[1, at : at + chunk, :] += src

    def last_rows(si):
        return None if si == HALF else rows - chunk if si > HALF else 0

    for si in range(ANG):
        packed_rows(si, PAD, PAD + rows)
        for at in range(0, rows, chunk):
            if at != last_rows(si):
                packed_step(si, at)
    arrive(row_copies[2:])

    def edge_pass(ti, carry):
        tscale = 0.5 * (ti - HALF).astype(F32)
        for sign, at in ((1, rows - chunk), (-1, 0)):
            sums = [[acc[ti, f, h, at : at + chunk, :] for h in range(2)] for f in range(2)]
            middle = [cen[ti, h, at : at + chunk, :] for h in range(2)]
            for size in range(1, HALF + 1):
                slot = 2 * (size - 1) + (sign < 0)
                low = PAD + at if sign > 0 else 0
                widen(ti, slot, sign * size, low, low + 2 * PAD)
                view_step(ti, tscale, slot, sign * size, at, middle, sums)
            for f in range(2):
                for h in range(2):
                    acc[ti, f, h, at : at + chunk, :] = sums[f][h]
        return carry

    lax.fori_loop(0, ANG, edge_pass, 0)
    for si in range(ANG):
        if si != HALF:
            low = PAD + rows if si > HALF else 0
            packed_rows(si, low, low + PAD)
            packed_step(si, last_rows(si))

    for f in range(2):
        ta, tb = acc[HALF, f, 0], acc[HALF, f, 1]
        for ti in range(ANG):
            m = D0 * abs(ti - HALF)
            if m == 0:
                continue
            a, b = acc[ti, f, 0], acc[ti, f, 1]
            g = m // D0 - 1
            if ti > HALF:
                ra, rb = roll(a, -m), roll(b, -m)
                ta = ta + jnp.where(lane < LANES - m, ra, rb)
                tb = tb + jnp.where(lane <= LANES - 2 - m, rb, roll(pacc[f], 126 - m - 16 * g))
            else:
                ra, rb = roll(a, m), roll(b, m)
                ta = ta + jnp.where(lane >= m + 1, ra, roll(pacc[f], m - 78 - 16 * g))
                tb = tb + jnp.where(lane >= m, rb, ra)
        own[f, :, 0:LANES] = ta
        own[f, :, LANES : 2 * LANES] = tb

    coeff = damping + own[0] * (1.0 / VIEWS)
    source = own[1] * (-1.0 / VIEWS)

    inner = (slice(8, 8 + rows), slice(LANES, LANES + cols))
    zed = source / (coeff + weights[inner])
    zc[0] = zed
    zc[1] = coeff
    gpack[0] = jnp.where(right_part, zed[:, 0:LANES], roll(coeff[:, 0:LANES], 64))
    gpack[1] = jnp.where(right_part, roll(coeff[:, cols - LANES : cols], 64), zed[:, cols - LANES : cols])

    copies2 = []
    for index, (dr, dc) in enumerate(DIRS):
        if dc == 0:
            src = zc.at[:, pl.ds(0, 8), :] if dr < 0 else zc.at[:, pl.ds(rows - 8, 8), :]
            dst = ghost_d if dr < 0 else ghost_u
        elif dr == 0:
            src = gpack.at[0] if dc < 0 else gpack.at[1]
            dst = ghost_r if dc < 0 else ghost_l
        else:
            src = gpack.at[0 if dc < 0 else 1, pl.ds(0 if dr < 0 else rows - 8, 8), :]
            dst = corner.at[index - 4]
        copies2.append((dr, dc, pltpu.make_async_remote_copy(
            src_ref=src, dst_ref=dst, send_sem=send2.at[index], recv_sem=recv2.at[index],
            device_id=(r + dr, c + dc), device_id_type=pl.DeviceIdType.MESH)))
    start(copies2)
    drain(row_copies + col_copies)
    arrive(copies2)

    zf = jnp.concatenate([
        jnp.concatenate([corner[3], ghost_u[0], corner[2]], axis=1),
        jnp.concatenate([ghost_l[...], zed, ghost_r[...]], axis=1),
        jnp.concatenate([corner[1], ghost_d[0], corner[0]], axis=1)], axis=0)
    one = jnp.ones((8, LANES), F32)
    kf = jnp.concatenate([
        jnp.concatenate([one, ghost_u[1], one], axis=1),
        jnp.concatenate([roll(ghost_l[...], 64), coeff, roll(ghost_r[...], 64)], axis=1),
        jnp.concatenate([one, ghost_d[1], one], axis=1)], axis=0)
    diag = kf + weights

    def operate(z):
        edges = edge_e * east(z) + edge_w * west(z) + edge_s * south(z) + edge_n * north(z)
        return diag * z - smooth_weight * edges

    wf = operate(zf)
    qf = wf / diag
    vf = operate(qf)
    w, q, v = wf[inner], qf[inner], vf[inner]
    rest = source - w
    y = zed - q
    wv = w - v
    sums = (zed * w, zed * rest, y * rest, q * rest, q * w, y * wv, y * v, q * v)
    line = lax.broadcasted_iota(jnp.int32, (1, LANES), 1)
    packed = jnp.zeros((1, LANES), F32)
    for i, x in enumerate(sums):
        x = jnp.sum(x, axis=0, keepdims=True)
        x = jnp.sum(x, axis=1, keepdims=True)
        packed = jnp.where(line == i, x, packed)
    redout[0] = packed
    redbuf[me] = packed

    def red_copy(i):
        peer = (me + i) % count
        return pltpu.make_async_remote_copy(
            src_ref=redout.at[0], dst_ref=redbuf.at[me], send_sem=rsend.at[0], recv_sem=rrecv.at[0],
            device_id=(peer // ncol, peer % ncol), device_id_type=pl.DeviceIdType.MESH)

    def cast_out(i, carry):
        red_copy(i).start()
        return carry

    lax.fori_loop(1, count, cast_out, 0)
    drain(copies2)
    others = redbuf.at[pl.ds(0, count - 1)]
    pltpu.make_async_copy(others, others, rrecv.at[0]).wait()
    pltpu.make_async_copy(others, others, rsend.at[0]).wait()
    totals = jnp.sum(redbuf[...], axis=0)
    b, e, f, g, h, k, l, m = [totals[:, i : i + 1] for i in range(8)]
    delta = e / b
    step0 = (e + b) / b
    rz0 = e + b
    rz1 = f - 2.0 * delta * g + delta * delta * h
    wu1 = k - 2.0 * delta * l + delta * delta * m
    beta = rz1 / rz0
    step1 = rz1 / (wu1 - beta * rz1 / step0)
    direction = (y - delta * q) + beta * zed
    image = (wv - delta * v) + beta * w
    out[0] = step0 * zed + step1 * direction
    out[1] = (source - step0 * w) - step1 * image


def solution(mesh):
    nrow, ncol = mesh.shape["row"], mesh.shape["col"]

    def shards(views):
        _, rows, cols = views.shape
        full = PAD + rows + PAD
        bf = views.dtype
        out = pl.pallas_call(
            functools.partial(kernel, nrow, ncol),
            out_shape=jax.ShapeDtypeStruct((2, rows, cols), F32),
            in_specs=[pl.BlockSpec(memory_space=pltpu.HBM)],
            out_specs=pl.BlockSpec(memory_space=pltpu.VMEM),
            scratch_shapes=[
                pltpu.VMEM((VIEWS, full, cols), bf),
                pltpu.VMEM((2, 5, rows, LANES), bf),
                pltpu.VMEM((5, full, LANES), bf),
                pltpu.VMEM((5, full, LANES), bf),
                pltpu.VMEM((8, 2, full, LANES), F32),
                pltpu.VMEM((ANG, full, LANES), F32),
                pltpu.VMEM((ANG, 2, rows, LANES), F32),
                pltpu.VMEM((rows, LANES), F32),
                pltpu.VMEM((ANG, 2, 2, rows, LANES), F32),
                pltpu.VMEM((2, rows, LANES), F32),
                pltpu.VMEM((2, rows, cols), F32),
                pltpu.VMEM((2, rows, cols), F32),
                pltpu.VMEM((2, rows, LANES), F32),
                pltpu.VMEM((2, 8, cols), F32),
                pltpu.VMEM((2, 8, cols), F32),
                pltpu.VMEM((rows, LANES), F32),
                pltpu.VMEM((rows, LANES), F32),
                pltpu.VMEM((4, 8, LANES), F32),
                pltpu.VMEM((nrow * ncol, 1, LANES), F32),
                pltpu.VMEM((1, 1, LANES), F32),
                pltpu.SemaphoreType.DMA((ANG,)),
                pltpu.SemaphoreType.DMA((16,)),
                pltpu.SemaphoreType.DMA((16,)),
                pltpu.SemaphoreType.DMA((8,)),
                pltpu.SemaphoreType.DMA((8,)),
                pltpu.SemaphoreType.DMA((1,)),
                pltpu.SemaphoreType.DMA((1,)),
            ],
            compiler_params=pltpu.CompilerParams(collective_id=0, has_side_effects=True, vmem_limit_bytes=48 << 20),
        )(pltpu.with_memory_space_constraint(views, pltpu.HBM))
        return out[0], out[1]

    return jax.shard_map(
        shards,
        mesh=mesh,
        in_specs=(P(None, "row", "col"),),
        out_specs=(P("row", "col"), P("row", "col")),
        check_vma=False,
    )
```
